768 devices in a mesh: row: 32 (over z_hi, y), col: 24 (over z_lo, x, core).
Axes of the slice: x: 4, y: 8, z: 12 (z_hi: 4, z_lo: 3; z = z_hi * 3 + z_lo), core: 2. Of those that a mesh axis runs over, the one named last changes fastest.
Arguments:
- start_vectors: float32 [16, 98304], P(None, ('col', 'row')), may hold values from -6 to 6
- tile_values: bfloat16 [32, 24, 8, 128, 128], P('row', 'col'), may hold values from -6 to 6
- tile_scales: float32 [32, 24, 8], P('row', 'col'), may hold values from 0.5 to 2
- tile_rows: int32 [32, 24, 8], P('row', 'col'), may hold values from 0 to 23
- tile_cols: int32 [32, 24, 8], P('row', 'col'), may hold values from 0 to 31
- tile_counts: int32 [32, 24], P('row', 'col'), may hold values from 2 to 8, as said below
Outputs:
- filtered: float32 [16, 98304], P(None, ('col', 'row'))
The draws below stay inside these ranges and needn't reach their ends.
Inputs may be any that keep to these rules, and one draw needn't show every extreme that they name: `tile_counts`: each device holds between 2 and 8 live tiles; some device holds exactly 8.
All inputs are finite; a program needn't handle non-finite values.
Results may differ from the reference program's by a relative error of at most 0.0037.
Values may be sent and summed in bfloat16 or wider, within the bound.
No kernel may reach another device: no remote copies, remote signals or barrier semaphores. Data moves between devices by JAX's collectives and lax.ppermute only.
A program may use at most 32 MiB of HBM per device.

```python
import math
import jax
import jax.numpy as jnp
from jax import lax

BLK = 128
VECS = 16
TILES = 8
STEPS = 2
NS = 98304
N_ROW = 32
N_COL = 24


def draw_tile_counts(key, part):
    first_key, second_key, third_key = jax.random.split(jax.random.fold_in(key, 7), 3)
    counts = jax.random.randint(first_key, (N_ROW, N_COL), TILES // 4, TILES + 1, dtype=jnp.int32)
    row_pick = jax.random.randint(second_key, (), 0, N_ROW, dtype=jnp.int32)
    col_pick = jax.random.randint(third_key, (), 0, N_COL, dtype=jnp.int32)
    return counts.at[row_pick, col_pick].set(TILES)


def touch_ends(result, key, smallest, high):
    place = [jax.random.randint(jax.random.fold_in(key, axis), (), 0, length) for axis, length in enumerate(result.shape)]
    longest = result.shape.index(max(result.shape))
    beside = place[:longest] + [(place[longest] + 1) % result.shape[longest]] + place[longest + 1:]
    return result.at[tuple(place)].set(smallest).at[tuple(beside)].set(high)


def block_levels(own_key, dims, pieces, least, top_value):
    loudness, own = 1.0, jax.random.fold_in(own_key, 6)
    for position, blocks in pieces:
        steps = jnp.exp(jax.random.uniform(jax.random.fold_in(own, position), (blocks,), jnp.float32, least / len(pieces), top_value / len(pieces)))
        loudness = loudness * jnp.repeat(steps, dims[position] // blocks).reshape([-1 if axis == position else 1 for axis in range(len(dims))])
    return loudness


def gaussian(own_key, extent, scale, most, shards=(), kind=jnp.bfloat16):
    result = jax.random.normal(own_key, extent, jnp.float32) * scale
    if len(shards) > 0:
        result = block_levels(own_key, extent, shards, -0.22, 0.18) * result
    return jnp.clip(result, min=-most, max=most).astype(kind)


def setup_inputs(seed: int = 0) -> dict:
    key_list = jax.random.split(jax.random.key(seed), 7)
    start_vectors = gaussian(key_list[0], (VECS, NS), 1.0, 6.0, ((1, 768),), jnp.float32)
    tile_values = gaussian(key_list[1], (N_ROW, N_COL, TILES, BLK, BLK), 1.0, 6.0, ((0, 32), (1, 24)))
    tile_scales = jnp.clip(jnp.exp(math.log(2.0) - 1.3862944 * jax.random.uniform(key_list[2], (N_ROW, N_COL, TILES), jnp.float32) ** block_levels(key_list[2], (N_ROW, N_COL, TILES), ((0, 32), (1, 24)), -0.2, 0.2)), 0.5, 2.0)
    tile_rows = touch_ends(jax.random.randint(key_list[3], (N_ROW, N_COL, TILES), 0, N_COL), jax.random.fold_in(key_list[3], 1), 0, N_COL - 1).astype(jnp.int32)
    tile_cols = touch_ends(jax.random.randint(key_list[4], (N_ROW, N_COL, TILES), 0, N_ROW), jax.random.fold_in(key_list[4], 1), 0, N_ROW - 1).astype(jnp.int32)
    tile_counts = draw_tile_counts(jax.random.fold_in(key_list[6], 71), 0)
    return {"start_vectors": start_vectors, "tile_values": tile_values, "tile_scales": tile_scales, "tile_rows": tile_rows, "tile_cols": tile_cols, "tile_counts": tile_counts}


def apply_operator(current, tile_values, tile_scales, tile_rows, tile_cols, tile_counts):
    device_total = N_ROW * N_COL
    rounded = lax.optimization_barrier(current.astype(jnp.bfloat16))
    blocks = rounded.astype(jnp.float32).reshape(VECS, device_total, BLK)
    flat_values = tile_values.reshape(device_total, TILES, BLK, BLK)
    flat_scales = tile_scales.reshape(device_total, TILES)
    flat_rows = tile_rows.reshape(device_total, TILES)
    flat_cols = tile_cols.reshape(device_total, TILES)
    flat_counts = tile_counts.reshape(device_total)
    device_ids = jnp.arange(device_total, dtype=jnp.int32)
    slot_ids = jnp.arange(TILES, dtype=jnp.int32)

    def visit(accum, items):
        tile_vals, scales, rows, cols, count, device = items
        row_group = device // N_COL
        col_group = device % N_COL
        row_block = (rows * N_ROW + row_group).astype(jnp.int32)
        col_block = (col_group * N_ROW + cols).astype(jnp.int32)
        weight = scales * (slot_ids < count).astype(jnp.float32)
        values_wide = tile_vals.astype(jnp.float32)
        direct = jnp.einsum('vtk,tjk->vtj', blocks[:, col_block], values_wide, precision=lax.Precision.HIGHEST)
        flipped = jnp.einsum('vtj,tjk->vtk', blocks[:, row_block], values_wide, precision=lax.Precision.HIGHEST)
        direct = direct * weight[None, :, None]
        flipped = flipped * weight[None, :, None]
        accum = accum.at[:, row_block].add(direct).at[:, col_block].add(flipped)
        return (accum, None)
    start = jnp.zeros((VECS, device_total, BLK), jnp.float32)
    accum, unused = lax.scan(visit, start, (flat_values, flat_scales, flat_rows, flat_cols, flat_counts, device_ids))
    factor = 0.5 / jnp.sqrt(jnp.float32(2.0 * TILES * BLK))
    return factor * accum.reshape(VECS, NS)

def reference(start_vectors, tile_values, tile_scales, tile_rows, tile_cols, tile_counts):
    previous = start_vectors
    current = apply_operator(start_vectors, tile_values, tile_scales, tile_rows, tile_cols, tile_counts)
    for repeat in range(STEPS - 1):
        following = 2.0 * apply_operator(current, tile_values, tile_scales, tile_rows, tile_cols, tile_counts) - previous
        previous = current
        current = following
    return current
```

```python
import functools
import math

import jax
import jax.numpy as jnp
from jax import lax
from jax.experimental import pallas as pl
from jax.experimental.pallas import tpu as pltpu
from jax.sharding import PartitionSpec as P


def product_kernel(flipped, count_ref, scale_ref, from_ref, to_ref, blocks_ref, tiles_ref, out_ref, acc_ref):
    acc_ref[...] = jnp.zeros_like(acc_ref)
    for slot in range(tiles_ref.shape[0]):
        weight = jnp.where(slot < count_ref[0], scale_ref[slot], 0.0)
        contracted = 0 if flipped else 1
        product = lax.dot_general(
            blocks_ref[from_ref[slot]],
            tiles_ref[slot],
            (((1,), (contracted,)), ((), ())),
            preferred_element_type=jnp.float32,
        )
        target = to_ref[slot]
        acc_ref[target] = acc_ref[target] + product * weight
    out_ref[...] = acc_ref[...].astype(out_ref.dtype)


def products(blocks, tile_vals, count, scales, source, target, groups, flipped):
    vec_count, width = blocks.shape[1:]
    smem = pl.BlockSpec(memory_space=pltpu.SMEM)
    vmem = pl.BlockSpec(memory_space=pltpu.VMEM)
    slots = tile_vals.shape[0]
    return pl.pallas_call(
        functools.partial(product_kernel, flipped),
        out_shape=jax.ShapeDtypeStruct((groups, vec_count, width), jnp.bfloat16),
        in_specs=[smem, smem, smem, smem, vmem, vmem],
        out_specs=vmem,
        scratch_shapes=[pltpu.VMEM((groups, vec_count, width), jnp.float32)],
        cost_estimate=pl.CostEstimate(
            flops=2 * slots * vec_count * width * width, bytes_accessed=2 * tile_vals.size, transcendentals=0
        ),
        name="flipped" if flipped else "direct",
    )(count, scales, source, target, blocks, tile_vals)


def body(start_vectors, tile_values, tile_scales, tile_rows, tile_cols, tile_counts):
    tile_vals = tile_values[0, 0]
    scales = tile_scales[0, 0]
    row_index = tile_rows[0, 0]
    col_index = tile_cols[0, 0]
    count = tile_counts[0]
    total, tile_width = tile_vals.shape[:2]
    factor = 0.5 / math.sqrt(2.0 * total * tile_width)
    row_size = lax.axis_size("row")
    col_size = lax.axis_size("col")

    def everywhere(block, size):
        return jnp.broadcast_to(block[None], (size, *block.shape))

    def exchange(blocks, axis):
        return lax.all_to_all(blocks, axis, 0, 0, tiled=True)

    def operate(current):
        rounded = current.astype(jnp.bfloat16)
        row_blocks = exchange(everywhere(rounded, col_size), "col")
        transposed = products(row_blocks, tile_vals, count, scales, row_index, col_index, row_size, True)
        col_blocks = exchange(everywhere(rounded, row_size), "row")
        direct = products(col_blocks, tile_vals, count, scales, col_index, row_index, col_size, False)
        from_col = jnp.sum(exchange(direct, "col"), axis=0, dtype=jnp.float32)
        from_row = jnp.sum(exchange(transposed, "row"), axis=0, dtype=jnp.float32)
        return factor * (from_col + from_row)

    following = operate(start_vectors)
    return 2.0 * operate(following) - start_vectors


def solution(mesh):
    in_specs = (
        P(None, ("col", "row")),
        P("row", "col", None, None, None),
        P("row", "col", None),
        P("row", "col", None),
        P("row", "col", None),
        P("row", "col"),
    )
    out_specs = P(None, ("col", "row"))
    return jax.shard_map(body, mesh=mesh, in_specs=in_specs, out_specs=out_specs, check_vma=False)
```

```python
import functools
import math

import jax
import jax.numpy as jnp
from jax import lax
from jax.experimental import pallas as pl
from jax.experimental.pallas import tpu as pltpu
from jax.sharding import Mesh
from jax.sharding import PartitionSpec as P


def product_kernel(flipped, count_ref, scale_ref, row_ref, col_ref, blocks_ref, tiles_ref, out_ref, acc_ref):
    acc_ref[...] = jnp.zeros_like(acc_ref)
    cores, slots = tiles_ref.shape[:2]
    for core in range(cores):
        for slot in range(slots):
            weight = jnp.where(slot < count_ref[core], scale_ref[core, slot], 0.0)
            row = row_ref[core, slot]
            col = col_ref[core, slot] * cores + core
            source, target, contracted = (row, col, 0) if flipped else (col, row, 1)
            product = lax.dot_general(
                blocks_ref[source],
                tiles_ref[core, slot],
                (((1,), (contracted,)), ((), ())),
                preferred_element_type=jnp.float32,
            )
            acc_ref[target] = acc_ref[target] + product * weight
    out_ref[...] = acc_ref[...].astype(out_ref.dtype)


def products(blocks, tile_vals, count, scales, rows, cols, groups, flipped):
    vec_count, width = blocks.shape[1:]
    smem = pl.BlockSpec(memory_space=pltpu.SMEM)
    vmem = pl.BlockSpec(memory_space=pltpu.VMEM)
    return pl.pallas_call(
        functools.partial(product_kernel, flipped),
        out_shape=jax.ShapeDtypeStruct((groups, vec_count, width), jnp.bfloat16),
        in_specs=[smem, smem, smem, smem, vmem, vmem],
        out_specs=vmem,
        scratch_shapes=[pltpu.VMEM((groups, vec_count, width), jnp.float32)],
        cost_estimate=pl.CostEstimate(
            flops=2 * vec_count * tile_vals.size, bytes_accessed=2 * tile_vals.size, transcendentals=0
        ),
        name="flipped" if flipped else "direct",
    )(count, scales, rows, cols, blocks, tile_vals)


def body(start_vectors, tile_values, tile_scales, tile_rows, tile_cols, tile_counts):
    total, tile_width = tile_values.shape[2:4]
    vec_count = start_vectors.shape[0]
    factor = 0.5 / math.sqrt(2.0 * total * tile_width)
    row_size = lax.axis_size("row")
    pair_size = lax.axis_size("pair")
    core_size = lax.axis_size("core")
    core = lax.axis_index("core")

    def both_cores(array):
        return lax.all_gather(array, "core", axis=0, tiled=True)

    tile_vals = both_cores(tile_values[0])
    scales = both_cores(tile_scales[0])
    rows = both_cores(tile_rows[0])
    cols = both_cores(tile_cols[0])
    count = both_cores(tile_counts[0])

    def exchange(blocks, axis):
        return lax.all_to_all(blocks, axis, 0, 0, tiled=True)

    def fetch(blocks, axis, size):
        got = exchange(jnp.broadcast_to(blocks[None], (size, *blocks.shape)), axis)
        return got.reshape(size * core_size, vec_count, tile_width)

    def give(partial, axis, size):
        got = exchange(partial.reshape(size, core_size, vec_count, tile_width), axis)
        return jnp.sum(got, axis=0, dtype=jnp.float32)

    def flipped_chain(blocks):
        row_blocks = fetch(blocks, "pair", pair_size)
        partial = products(row_blocks, tile_vals, count, scales, rows, cols, row_size * core_size, True)
        return give(partial, "row", row_size)

    def direct_chain(blocks):
        col_blocks = fetch(blocks, "row", row_size)
        partial = products(col_blocks, tile_vals, count, scales, rows, cols, pair_size * core_size, False)
        return give(partial, "pair", pair_size)

    def operate(blocks):
        mine = lax.cond(core == 0, flipped_chain, direct_chain, blocks)
        return factor * jnp.sum(both_cores(mine[None]), axis=0)

    following = operate(both_cores(start_vectors.astype(jnp.bfloat16)[None]))
    last = operate(following.astype(jnp.bfloat16))
    return 2.0 * lax.dynamic_index_in_dim(last, core, 0, keepdims=False) - start_vectors


def solution(mesh):
    rows, cols = mesh.devices.shape
    split = Mesh(mesh.devices.reshape(rows, cols // 2, 2), ("row", "pair", "core"))
    columns = ("pair", "core")
    in_specs = (
        P(None, (*columns, "row")),
        P("row", columns, None, None, None),
        P("row", columns, None),
        P("row", columns, None),
        P("row", columns, None),
        P("row", columns),
    )
    out_specs = P(None, (*columns, "row"))
    return jax.shard_map(body, mesh=split, in_specs=in_specs, out_specs=out_specs, check_vma=False)
```

```python
import functools
import math

import jax
import jax.numpy as jnp
from jax import lax
from jax.experimental import pallas as pl
from jax.experimental.pallas import tpu as pltpu
from jax.sharding import Mesh
from jax.sharding import PartitionSpec as P

VMEM_LIMIT = 8 << 20
SMEM_BLOCK = pl.BlockSpec(memory_space=pltpu.SMEM)
VMEM_BLOCK = pl.BlockSpec(memory_space=pltpu.VMEM)


def pack_kernel(count_ref, start_ref, row_ref, col_ref, scale_ref, out_ref):
    vec_count, slots = start_ref.shape[0], row_ref.shape[1]
    out_ref[:vec_count] = start_ref[...]
    out_ref[vec_count:] = jnp.zeros_like(out_ref[vec_count:])
    slot = lax.broadcasted_iota(jnp.int32, (1, slots), 1)
    out_ref[vec_count : vec_count + 1, :slots] = row_ref[...].astype(jnp.float32)
    out_ref[vec_count + 1 : vec_count + 2, :slots] = col_ref[...].astype(jnp.float32)
    out_ref[vec_count + 2 : vec_count + 3, :slots] = jnp.where(slot < count_ref[0], scale_ref[...], 0.0)


def pack(start, rows, cols, scales, count):
    vec_count, width = start.shape
    return pl.pallas_call(
        pack_kernel,
        out_shape=jax.ShapeDtypeStruct((vec_count + 8, width), jnp.float32),
        in_specs=[SMEM_BLOCK, VMEM_BLOCK, VMEM_BLOCK, VMEM_BLOCK, VMEM_BLOCK],
        out_specs=VMEM_BLOCK,
        compiler_params=pltpu.CompilerParams(vmem_limit_bytes=VMEM_LIMIT),
        name="pack",
    )(count, start, rows, cols, scales)


def product_kernel(flipped, row_shift, row_size, pair_shift, pair_size, packed_ref, blocks_ref, tiles_ref, out_ref, acc_ref):
    acc_ref[...] = jnp.zeros_like(acc_ref)
    cores, slots = tiles_ref.shape[:2]
    stride = packed_ref.shape[0] // cores
    for core in range(cores):
        base = core * stride + blocks_ref.shape[1]
        for slot in range(slots):
            row = packed_ref[base, slot].astype(jnp.int32)
            col = packed_ref[base + 1, slot].astype(jnp.int32)
            weight = packed_ref[base + 2, slot]
            row = lax.rem(row + pair_shift * cores, pair_size * cores)
            col = lax.rem(col + row_shift, row_size) * cores + core
            source, target, contracted = (row, col, 0) if flipped else (col, row, 1)
            product = lax.dot_general(
                blocks_ref[source],
                tiles_ref[core, slot],
                (((1,), (contracted,)), ((), ())),
                preferred_element_type=jnp.float32,
            )
            acc_ref[target] = acc_ref[target] + product * weight
    out_ref[...] = acc_ref[...].astype(out_ref.dtype)


def body(row_lead, pair_lead, start_vectors, tile_values, tile_scales, tile_rows, tile_cols, tile_counts):
    total, tile_width = tile_values.shape[2:4]
    vec_count = start_vectors.shape[0]
    factor = 0.5 / math.sqrt(2.0 * total * tile_width)
    size = {axis: lax.axis_size(axis) for axis in ("row", "pair")}
    cores = lax.axis_size("core")
    lead = {"row": row_lead, "pair": pair_lead}
    shift = {axis: size[axis] - lead[axis] for axis in size}
    core = lax.axis_index("core")

    def both_cores(array):
        return lax.all_gather(array, "core", axis=0, tiled=True)

    packed = both_cores(pack(start_vectors, tile_rows[0], tile_cols[0], tile_scales[0], tile_counts[0]))
    tile_vals = both_cores(tile_values[0])

    def exchange(blocks, axis):
        order = [(lead[axis] + i) % size[axis] for i in range(size[axis])]
        return lax.all_to_all(blocks, axis, 0, 0, tiled=True, axis_index_groups=[order])

    def products(blocks, groups, flipped):
        kernel = functools.partial(
            product_kernel, flipped, shift["row"], size["row"], shift["pair"], size["pair"]
        )
        return pl.pallas_call(
            kernel,
            out_shape=jax.ShapeDtypeStruct((groups, vec_count, tile_width), jnp.bfloat16),
            in_specs=[SMEM_BLOCK, VMEM_BLOCK, VMEM_BLOCK],
            out_specs=VMEM_BLOCK,
            scratch_shapes=[pltpu.VMEM((groups, vec_count, tile_width), jnp.float32)],
            compiler_params=pltpu.CompilerParams(vmem_limit_bytes=VMEM_LIMIT),
            name="flipped" if flipped else "direct",
        )(packed, blocks, tile_vals)

    def chain(out_axis, back_axis, flipped, make_blocks, operand):
        blocks = make_blocks(operand).astype(jnp.bfloat16)
        got = exchange(jnp.broadcast_to(blocks[None], (size[out_axis], *blocks.shape)), out_axis)
        got = got.reshape(size[out_axis] * cores, vec_count, tile_width)
        partial = products(got, size[back_axis] * cores, flipped)
        parts = exchange(partial.reshape(size[back_axis], cores, vec_count, tile_width), back_axis)
        return jnp.sum(parts, axis=0, dtype=jnp.float32)

    def operate(make_blocks, operand):
        mine = lax.cond(
            core == 0,
            functools.partial(chain, "pair", "row", True, make_blocks),
            functools.partial(chain, "row", "pair", False, make_blocks),
            operand,
        )
        return both_cores(mine).reshape(2, cores, vec_count, tile_width)

    def start_blocks(array):
        return array.reshape(cores, -1, tile_width)[:, :vec_count]

    def next_blocks(parts):
        return factor * (parts[0] + parts[1])

    parts = operate(start_blocks, packed)
    parts = operate(next_blocks, parts)
    mine = lax.dynamic_index_in_dim(parts, core, 1, keepdims=False)
    return 2.0 * factor * (mine[0] + mine[1]) - start_vectors


def solution(mesh):
    rows, cols = mesh.devices.shape
    pairs = cols // 2
    split = Mesh(mesh.devices.reshape(rows, pairs, 2), ("row", "pair", "core"))
    columns = ("pair", "core")
    in_specs = (
        P(None, (*columns, "row")),
        P("row", columns, None, None, None),
        P("row", columns, None),
        P("row", columns, None),
        P("row", columns, None),
        P("row", columns),
    )
    out_specs = P(None, (*columns, "row"))
    step = functools.partial(body, rows * 5 // 8, pairs // 3)
    return jax.shard_map(step, mesh=split, in_specs=in_specs, out_specs=out_specs, check_vma=False)
```

```python
import functools
import math

import jax
import jax.numpy as jnp
from jax import lax
from jax.experimental import pallas as pl
from jax.experimental.pallas import tpu as pltpu
from jax.sharding import Mesh
from jax.sharding import PartitionSpec as P

VMEM_LIMIT = 8 << 20
PACK_LIMIT = 60 << 20
META = 16
LEADS = (4, 20, 18, 4)
SMEM_BLOCK = pl.BlockSpec(memory_space=pltpu.SMEM)
VMEM_BLOCK = pl.BlockSpec(memory_space=pltpu.VMEM)
HBM_BLOCK = pl.BlockSpec(memory_space=pltpu.HBM)


def pack_kernel(count_in, start_in, row_in, col_in, scale_in, tile_in, out_ref, count, start, row, col, scale, sems):
    vec_count, slots = start_in.shape[0], row_in.shape[-1]
    pairs = (
        (count_in, count),
        (start_in, start),
        (row_in, row),
        (col_in, col),
        (scale_in, scale),
        (tile_in, out_ref.at[pl.ds(vec_count + META, tile_in.shape[0])]),
    )
    copies = [pltpu.make_async_copy(source, target, sems.at[i]) for i, (source, target) in enumerate(pairs)]
    for copy in copies:
        copy.start()
    for copy in copies[:-1]:
        copy.wait()
    slot = lax.broadcasted_iota(jnp.int32, (1, slots), 1)
    weight = jnp.where(slot < count[0, 0], scale[...], 0.0)
    high = weight.astype(jnp.bfloat16).astype(jnp.float32)
    middle = (weight - high).astype(jnp.bfloat16).astype(jnp.float32)
    low = weight - high - middle
    lines = [row[...].astype(jnp.float32), col[...].astype(jnp.float32), high, middle, low]
    lines = jnp.concatenate([*lines, jnp.zeros((META - len(lines), slots), jnp.float32)], axis=0)
    out_ref[:vec_count] = start[...].astype(jnp.bfloat16)
    out_ref[vec_count : vec_count + META] = jnp.zeros((META, out_ref.shape[1]), jnp.bfloat16)
    out_ref[vec_count : vec_count + META, :slots] = lines.astype(jnp.bfloat16)
    copies[-1].wait()


def pack(start, rows, cols, scales, count, tiles):
    vec_count, width = start.shape
    slots = tiles.shape[0]
    return pl.pallas_call(
        pack_kernel,
        out_shape=jax.ShapeDtypeStruct((vec_count + META + slots * width, width), jnp.bfloat16),
        in_specs=[HBM_BLOCK] * 6,
        out_specs=VMEM_BLOCK,
        scratch_shapes=[
            pltpu.SMEM((1, 1), jnp.int32),
            pltpu.VMEM((vec_count, width), jnp.float32),
            pltpu.VMEM((1, slots), jnp.int32),
            pltpu.VMEM((1, slots), jnp.int32),
            pltpu.VMEM((1, slots), jnp.float32),
            pltpu.SemaphoreType.DMA((6,)),
        ],
        compiler_params=pltpu.CompilerParams(vmem_limit_bytes=PACK_LIMIT),
        name="pack",
    )(count, start, rows, cols, scales, tiles.reshape(slots * width, width))


def unpack_kernel(shifts, packed_ref, start_ref, place_ref, weight_ref, kept_ref):
    cores, vec_count = packed_ref.shape[0], start_ref.shape[0]
    kept_ref[...] = start_ref[...]
    for core in range(cores):
        lines = packed_ref[core, vec_count : vec_count + META].astype(jnp.float32)
        row = lines[0:1].astype(jnp.int32)
        col = lines[1:2].astype(jnp.int32) * cores + core
        for i, (index, (shift, size)) in enumerate(zip((row, col, col, row), shifts)):
            place = index + shift * cores
            line = len(shifts) * core + i
            place_ref[line : line + 1] = jnp.where(place >= size * cores, place - size * cores, place)
        weight_ref[core : core + 1] = lines[2:3] + lines[3:4] + lines[4:5]


def product_kernel(flipped, slots, place_ref, weight_ref, packed_ref, blocks_ref, out_ref, acc_ref):
    acc_ref[...] = jnp.zeros_like(acc_ref)
    cores, _, width = packed_ref.shape
    first = blocks_ref.shape[1] + META
    for core in range(cores):
        for slot in range(slots):
            line = 4 * core + (0 if flipped else 2)
            source = place_ref[line, slot]
            target = place_ref[line + 1, slot]
            product = lax.dot_general(
                blocks_ref[source],
                packed_ref[core, first + slot * width : first + (slot + 1) * width],
                (((1,), (0 if flipped else 1,)), ((), ())),
                preferred_element_type=jnp.float32,
            )
            acc_ref[target] = acc_ref[target] + product * weight_ref[core, slot]
    out_ref[...] = acc_ref[...].astype(out_ref.dtype)


def body(leads, start_vectors, tile_values, tile_scales, tile_rows, tile_cols, tile_counts):
    total, tile_width = tile_values.shape[2:4]
    vec_count = start_vectors.shape[0]
    factor = 0.5 / math.sqrt(2.0 * total * tile_width)
    size = {axis: lax.axis_size(axis) for axis in ("row", "pair")}
    cores = lax.axis_size("core")
    axes = ("pair", "row", "row", "pair")
    shifts = tuple((size[axis] - lead, size[axis]) for axis, lead in zip(axes, leads))
    core = lax.axis_index("core")

    def both_cores(array):
        return lax.all_gather(array, "core", axis=0, tiled=True)

    packed = both_cores(
        pack(start_vectors, tile_rows[0], tile_cols[0], tile_scales[0], tile_counts, tile_values[0, 0])[None]
    )
    place, weight, kept = pl.pallas_call(
        functools.partial(unpack_kernel, shifts),
        out_shape=(
            jax.ShapeDtypeStruct((len(axes) * cores, tile_width), jnp.int32),
            jax.ShapeDtypeStruct((cores, tile_width), jnp.float32),
            jax.ShapeDtypeStruct(start_vectors.shape, jnp.float32),
        ),
        in_specs=[VMEM_BLOCK, VMEM_BLOCK],
        out_specs=(VMEM_BLOCK, VMEM_BLOCK, VMEM_BLOCK),
        compiler_params=pltpu.CompilerParams(vmem_limit_bytes=VMEM_LIMIT),
        name="unpack",
    )(packed, start_vectors)

    def exchange(blocks, leg):
        axis, lead = axes[leg], leads[leg]
        order = [(lead + i) % size[axis] for i in range(size[axis])]
        return lax.all_to_all(blocks, axis, 0, 0, tiled=True, axis_index_groups=[order])

    def products(blocks, groups, flipped):
        return pl.pallas_call(
            functools.partial(product_kernel, flipped, total),
            out_shape=jax.ShapeDtypeStruct((groups, vec_count, tile_width), jnp.bfloat16),
            in_specs=[SMEM_BLOCK, SMEM_BLOCK, VMEM_BLOCK, VMEM_BLOCK],
            out_specs=VMEM_BLOCK,
            scratch_shapes=[pltpu.VMEM((groups, vec_count, tile_width), jnp.float32)],
            compiler_params=pltpu.CompilerParams(vmem_limit_bytes=VMEM_LIMIT),
            name="flipped" if flipped else "direct",
        )(place, weight, packed, blocks)

    def chain(leg, make_blocks, operand):
        out_size, back_size = size[axes[leg]], size[axes[leg + 1]]
        blocks = make_blocks(operand).astype(jnp.bfloat16)
        got = exchange(jnp.broadcast_to(blocks[None], (out_size, *blocks.shape)), leg)
        partial = products(got.reshape(out_size * cores, vec_count, tile_width), back_size * cores, leg == 0)
        parts = exchange(partial.reshape(back_size, cores, vec_count, tile_width), leg + 1)
        return jnp.sum(parts, axis=0, dtype=jnp.float32)

    def operate(make_blocks, operand):
        mine = lax.cond(
            core == 0,
            functools.partial(chain, 0, make_blocks),
            functools.partial(chain, 2, make_blocks),
            operand,
        )
        return both_cores(mine).reshape(2, cores, vec_count, tile_width)

    def start_blocks(array):
        return array[:, :vec_count]

    def next_blocks(parts):
        return factor * (parts[0] + parts[1])

    parts = operate(start_blocks, packed)
    parts = operate(next_blocks, parts)
    mine = lax.dynamic_index_in_dim(parts, core, 1, keepdims=False)
    return 2.0 * factor * (mine[0] + mine[1]) - kept


def solution(mesh):
    rows, cols = mesh.devices.shape
    pairs = cols // 2
    split = Mesh(mesh.devices.reshape(rows, pairs, 2), ("row", "pair", "core"))
    columns = ("pair", "core")
    in_specs = (
        P(None, (*columns, "row")),
        P("row", columns, None, None, None),
        P("row", columns, None),
        P("row", columns, None),
        P("row", columns, None),
        P("row", columns),
    )
    out_specs = P(None, (*columns, "row"))
    step = functools.partial(body, LEADS)
    return jax.shard_map(step, mesh=split, in_specs=in_specs, out_specs=out_specs, check_vma=False)
```

```python
import functools
import math

import jax
import jax.numpy as jnp
from jax import lax
from jax.experimental import pallas as pl
from jax.experimental.pallas import tpu as pltpu
from jax.sharding import Mesh
from jax.sharding import PartitionSpec as P

VMEM_LIMIT = 8 << 20
PACK_LIMIT = 8 << 20
META = 16
LEADS = (4, 20, 18, 4)
SMEM_BLOCK = pl.BlockSpec(memory_space=pltpu.SMEM)
VMEM_BLOCK = pl.BlockSpec(memory_space=pltpu.VMEM)
HBM_BLOCK = pl.BlockSpec(memory_space=pltpu.HBM)


def pack_kernel(count_in, start_in, row_in, col_in, scale_in, tile_in, out_ref, count, start, row, col, scale, sems):
    vec_count, slots = start_in.shape[0], row_in.shape[-1]
    pairs = (
        (count_in, count),
        (start_in, start),
        (row_in, row),
        (col_in, col),
        (scale_in, scale),
        (tile_in, out_ref.at[pl.ds(vec_count + META, tile_in.shape[0])]),
    )
    copies = [pltpu.make_async_copy(source, target, sems.at[i]) for i, (source, target) in enumerate(pairs)]
    for copy in copies:
        copy.start()
    for copy in copies[:-1]:
        copy.wait()
    slot = lax.broadcasted_iota(jnp.int32, (1, slots), 1)
    weight = jnp.where(slot < count[0, 0], scale[...], 0.0)
    high = weight.astype(jnp.bfloat16).astype(jnp.float32)
    middle = (weight - high).astype(jnp.bfloat16).astype(jnp.float32)
    low = weight - high - middle
    lines = [row[...].astype(jnp.float32), col[...].astype(jnp.float32), high, middle, low]
    lines = jnp.concatenate([*lines, jnp.zeros((META - len(lines), slots), jnp.float32)], axis=0)
    out_ref[:vec_count] = start[...].astype(jnp.bfloat16)
    out_ref[vec_count : vec_count + META] = jnp.zeros((META, out_ref.shape[1]), jnp.bfloat16)
    out_ref[vec_count : vec_count + META, :slots] = lines.astype(jnp.bfloat16)
    copies[-1].wait()


def pack(start, rows, cols, scales, count, tiles):
    vec_count, width = start.shape
    slots = tiles.shape[0]
    arrays = (start, rows, cols, scales, tiles.reshape(slots * width, width))
    arrays = [pltpu.with_memory_space_constraint(array, pltpu.HBM) for array in arrays]
    return pl.pallas_call(
        pack_kernel,
        out_shape=jax.ShapeDtypeStruct((vec_count + META + slots * width, width), jnp.bfloat16),
        in_specs=[HBM_BLOCK] * 6,
        out_specs=VMEM_BLOCK,
        scratch_shapes=[
            pltpu.SMEM((1, 1), jnp.int32),
            pltpu.VMEM((vec_count, width), jnp.float32),
            pltpu.VMEM((1, slots), jnp.int32),
            pltpu.VMEM((1, slots), jnp.int32),
            pltpu.VMEM((1, slots), jnp.float32),
            pltpu.SemaphoreType.DMA((6,)),
        ],
        compiler_params=pltpu.CompilerParams(vmem_limit_bytes=PACK_LIMIT),
        name="pack",
    )(count, *arrays)


def unpack_kernel(shifts, packed_ref, start_ref, place_ref, weight_ref, kept_ref):
    cores, vec_count = packed_ref.shape[0], start_ref.shape[0]
    kept_ref[...] = start_ref[...]
    for core in range(cores):
        lines = packed_ref[core, vec_count : vec_count + META].astype(jnp.float32)
        row = lines[0:1].astype(jnp.int32)
        col = lines[1:2].astype(jnp.int32) * cores + core
        for i, (index, (shift, size)) in enumerate(zip((row, col, col, row), shifts)):
            place = index + shift * cores
            line = len(shifts) * core + i
            place_ref[line : line + 1] = jnp.where(place >= size * cores, place - size * cores, place)
        weight_ref[core : core + 1] = lines[2:3] + lines[3:4] + lines[4:5]


def product_kernel(flipped, slots, place_ref, weight_ref, packed_ref, blocks_ref, out_ref, acc_ref):
    acc_ref[...] = jnp.zeros_like(acc_ref)
    cores, _, width = packed_ref.shape
    first = blocks_ref.shape[1] + META
    for core in range(cores):
        for slot in range(slots):
            line = 4 * core + (0 if flipped else 2)
            source = place_ref[line, slot]
            target = place_ref[line + 1, slot]
            product = lax.dot_general(
                blocks_ref[source],
                packed_ref[core, first + slot * width : first + (slot + 1) * width],
                (((1,), (0 if flipped else 1,)), ((), ())),
                preferred_element_type=jnp.float32,
            )
            acc_ref[target] = acc_ref[target] + product * weight_ref[core, slot]
    out_ref[...] = acc_ref[...].astype(out_ref.dtype)


def body(leads, start_vectors, tile_values, tile_scales, tile_rows, tile_cols, tile_counts):
    total, tile_width = tile_values.shape[2:4]
    vec_count = start_vectors.shape[0]
    factor = 0.5 / math.sqrt(2.0 * total * tile_width)
    size = {axis: lax.axis_size(axis) for axis in ("row", "pair")}
    cores = lax.axis_size("core")
    axes = ("pair", "row", "row", "pair")
    shifts = tuple((size[axis] - lead, size[axis]) for axis, lead in zip(axes, leads))
    core = lax.axis_index("core")

    def both_cores(array):
        return lax.all_gather(array, "core", axis=0, tiled=True)

    packed = both_cores(
        pack(start_vectors, tile_rows[0], tile_cols[0], tile_scales[0], tile_counts, tile_values[0, 0])[None]
    )
    place, weight, kept = pl.pallas_call(
        functools.partial(unpack_kernel, shifts),
        out_shape=(
            jax.ShapeDtypeStruct((len(axes) * cores, tile_width), jnp.int32),
            jax.ShapeDtypeStruct((cores, tile_width), jnp.float32),
            jax.ShapeDtypeStruct(start_vectors.shape, jnp.float32),
        ),
        in_specs=[VMEM_BLOCK, VMEM_BLOCK],
        out_specs=(VMEM_BLOCK, VMEM_BLOCK, VMEM_BLOCK),
        compiler_params=pltpu.CompilerParams(vmem_limit_bytes=VMEM_LIMIT),
        name="unpack",
    )(packed, start_vectors)

    def exchange(blocks, leg):
        axis, lead = axes[leg], leads[leg]
        order = [(lead + i) % size[axis] for i in range(size[axis])]
        return lax.all_to_all(blocks, axis, 0, 0, tiled=True, axis_index_groups=[order])

    def products(blocks, groups, flipped):
        return pl.pallas_call(
            functools.partial(product_kernel, flipped, total),
            out_shape=jax.ShapeDtypeStruct((groups, vec_count, tile_width), jnp.bfloat16),
            in_specs=[SMEM_BLOCK, SMEM_BLOCK, VMEM_BLOCK, VMEM_BLOCK],
            out_specs=VMEM_BLOCK,
            scratch_shapes=[pltpu.VMEM((groups, vec_count, tile_width), jnp.float32)],
            compiler_params=pltpu.CompilerParams(vmem_limit_bytes=VMEM_LIMIT),
            name="flipped" if flipped else "direct",
        )(place, weight, packed, blocks)

    def chain(leg, make_blocks, operand):
        out_size, back_size = size[axes[leg]], size[axes[leg + 1]]
        blocks = make_blocks(operand).astype(jnp.bfloat16)
        got = exchange(jnp.broadcast_to(blocks[None], (out_size, *blocks.shape)), leg)
        partial = products(got.reshape(out_size * cores, vec_count, tile_width), back_size * cores, leg == 0)
        parts = exchange(partial.reshape(back_size, cores, vec_count, tile_width), leg + 1)
        return jnp.sum(parts, axis=0, dtype=jnp.float32)

    def operate(make_blocks, operand):
        mine = lax.cond(
            core == 0,
            functools.partial(chain, 0, make_blocks),
            functools.partial(chain, 2, make_blocks),
            operand,
        )
        return both_cores(mine).reshape(2, cores, vec_count, tile_width)

    def start_blocks(array):
        return array[:, :vec_count]

    def next_blocks(parts):
        return factor * (parts[0] + parts[1])

    parts = operate(start_blocks, packed)
    parts = operate(next_blocks, parts)
    mine = lax.dynamic_index_in_dim(parts, core, 1, keepdims=False)
    return 2.0 * factor * (mine[0] + mine[1]) - kept


def solution(mesh):
    rows, cols = mesh.devices.shape
    pairs = cols // 2
    split = Mesh(mesh.devices.reshape(rows, pairs, 2), ("row", "pair", "core"))
    columns = ("pair", "core")
    in_specs = (
        P(None, (*columns, "row")),
        P("row", columns, None, None, None),
        P("row", columns, None),
        P("row", columns, None),
        P("row", columns, None),
        P("row", columns),
    )
    out_specs = P(None, (*columns, "row"))
    step = functools.partial(body, LEADS)
    return jax.shard_map(step, mesh=split, in_specs=in_specs, out_specs=out_specs, check_vma=False)
```

```python
import functools
import math

import jax
import jax.numpy as jnp
from jax import lax
from jax.experimental import pallas as pl
from jax.experimental.pallas import tpu as pltpu
from jax.sharding import Mesh
from jax.sharding import PartitionSpec as P

VMEM_LIMIT = 8 << 20
PACK_LIMIT = 8 << 20
META = 16
LEADS = (4, 20, 13, 4)
SMEM_BLOCK = pl.BlockSpec(memory_space=pltpu.SMEM)
VMEM_BLOCK = pl.BlockSpec(memory_space=pltpu.VMEM)
HBM_BLOCK = pl.BlockSpec(memory_space=pltpu.HBM)


def pack_kernel(count_in, start_in, row_in, col_in, scale_in, tile_in, out_ref, count, start, row, col, scale, sems):
    vec_count, slots = start_in.shape[0], row_in.shape[-1]
    pairs = (
        (count_in, count),
        (start_in, start),
        (row_in, row),
        (col_in, col),
        (scale_in, scale),
        (tile_in, out_ref.at[pl.ds(vec_count + META, tile_in.shape[0])]),
    )
    copies = [pltpu.make_async_copy(source, target, sems.at[i]) for i, (source, target) in enumerate(pairs)]
    for copy in copies:
        copy.start()
    for copy in copies[:-1]:
        copy.wait()
    slot = lax.broadcasted_iota(jnp.int32, (1, slots), 1)
    weight = jnp.where(slot < count[0, 0], scale[...], 0.0)
    high = weight.astype(jnp.bfloat16).astype(jnp.float32)
    middle = (weight - high).astype(jnp.bfloat16).astype(jnp.float32)
    low = weight - high - middle
    lines = [row[...].astype(jnp.float32), col[...].astype(jnp.float32), high, middle, low]
    lines = jnp.concatenate([*lines, jnp.zeros((META - len(lines), slots), jnp.float32)], axis=0)
    out_ref[:vec_count] = start[...].astype(jnp.bfloat16)
    out_ref[vec_count : vec_count + META] = jnp.zeros((META, out_ref.shape[1]), jnp.bfloat16)
    out_ref[vec_count : vec_count + META, :slots] = lines.astype(jnp.bfloat16)
    copies[-1].wait()


def pack(start, rows, cols, scales, count, tiles):
    vec_count, width = start.shape
    slots = tiles.shape[0]
    arrays = (start, rows, cols, scales, tiles.reshape(slots * width, width))
    arrays = [pltpu.with_memory_space_constraint(array, pltpu.HBM) for array in arrays]
    return pl.pallas_call(
        pack_kernel,
        out_shape=jax.ShapeDtypeStruct((vec_count + META + slots * width, width), jnp.bfloat16),
        in_specs=[HBM_BLOCK] * 6,
        out_specs=VMEM_BLOCK,
        scratch_shapes=[
            pltpu.SMEM((1, 1), jnp.int32),
            pltpu.VMEM((vec_count, width), jnp.float32),
            pltpu.VMEM((1, slots), jnp.int32),
            pltpu.VMEM((1, slots), jnp.int32),
            pltpu.VMEM((1, slots), jnp.float32),
            pltpu.SemaphoreType.DMA((6,)),
        ],
        compiler_params=pltpu.CompilerParams(vmem_limit_bytes=PACK_LIMIT),
        name="pack",
    )(count, *arrays)


def unpack_kernel(shifts, packed_ref, start_ref, place_ref, weight_ref, kept_ref):
    cores, vec_count = packed_ref.shape[0], start_ref.shape[0]
    kept_ref[...] = start_ref[...]
    for core in range(cores):
        lines = packed_ref[core, vec_count : vec_count + META].astype(jnp.float32)
        row = lines[0:1].astype(jnp.int32)
        col = lines[1:2].astype(jnp.int32) * cores + core
        for i, (index, (shift, size)) in enumerate(zip((row, col, col, row), shifts)):
            place = index + shift * cores
            line = len(shifts) * core + i
            place_ref[line : line + 1] = jnp.where(place >= size * cores, place - size * cores, place)
        weight_ref[core : core + 1] = lines[2:3] + lines[3:4] + lines[4:5]


def product_kernel(flipped, slots, place_ref, weight_ref, packed_ref, blocks_ref, out_ref, acc_ref):
    acc_ref[...] = jnp.zeros_like(acc_ref)
    cores, _, width = packed_ref.shape
    first = blocks_ref.shape[1] + META
    for core in range(cores):
        for slot in range(slots):
            line = 4 * core + (0 if flipped else 2)
            source = place_ref[line, slot]
            target = place_ref[line + 1, slot]
            product = lax.dot_general(
                blocks_ref[source],
                packed_ref[core, first + slot * width : first + (slot + 1) * width],
                (((1,), (0 if flipped else 1,)), ((), ())),
                preferred_element_type=jnp.float32,
            )
            acc_ref[target] = acc_ref[target] + product * weight_ref[core, slot]
    out_ref[...] = acc_ref[...].astype(out_ref.dtype)


def body(leads, start_vectors, tile_values, tile_scales, tile_rows, tile_cols, tile_counts):
    total, tile_width = tile_values.shape[2:4]
    vec_count = start_vectors.shape[0]
    factor = 0.5 / math.sqrt(2.0 * total * tile_width)
    size = {axis: lax.axis_size(axis) for axis in ("row", "pair")}
    cores = lax.axis_size("core")
    axes = ("pair", "row", "row", "pair")
    shifts = tuple((size[axis] - lead, size[axis]) for axis, lead in zip(axes, leads))
    core = lax.axis_index("core")

    def both_cores(array):
        return lax.all_gather(array, "core", axis=0, tiled=True)

    packed = both_cores(
        pack(start_vectors, tile_rows[0], tile_cols[0], tile_scales[0], tile_counts, tile_values[0, 0])[None]
    )
    place, weight, kept = pl.pallas_call(
        functools.partial(unpack_kernel, shifts),
        out_shape=(
            jax.ShapeDtypeStruct((len(axes) * cores, tile_width), jnp.int32),
            jax.ShapeDtypeStruct((cores, tile_width), jnp.float32),
            jax.ShapeDtypeStruct(start_vectors.shape, jnp.float32),
        ),
        in_specs=[VMEM_BLOCK, VMEM_BLOCK],
        out_specs=(VMEM_BLOCK, VMEM_BLOCK, VMEM_BLOCK),
        compiler_params=pltpu.CompilerParams(vmem_limit_bytes=VMEM_LIMIT),
        name="unpack",
    )(packed, start_vectors)

    def exchange(blocks, leg):
        axis, lead = axes[leg], leads[leg]
        order = [(lead + i) % size[axis] for i in range(size[axis])]
        return lax.all_to_all(blocks, axis, 0, 0, tiled=True, axis_index_groups=[order])

    def products(blocks, groups, flipped):
        return pl.pallas_call(
            functools.partial(product_kernel, flipped, total),
            out_shape=jax.ShapeDtypeStruct((groups, vec_count, tile_width), jnp.bfloat16),
            in_specs=[SMEM_BLOCK, SMEM_BLOCK, VMEM_BLOCK, VMEM_BLOCK],
            out_specs=VMEM_BLOCK,
            scratch_shapes=[pltpu.VMEM((groups, vec_count, tile_width), jnp.float32)],
            compiler_params=pltpu.CompilerParams(vmem_limit_bytes=VMEM_LIMIT),
            name="flipped" if flipped else "direct",
        )(place, weight, packed, blocks)

    def chain(leg, make_blocks, operand):
        out_size, back_size = size[axes[leg]], size[axes[leg + 1]]
        blocks = make_blocks(operand).astype(jnp.bfloat16)
        got = exchange(jnp.broadcast_to(blocks[None], (out_size, *blocks.shape)), leg)
        partial = products(got.reshape(out_size * cores, vec_count, tile_width), back_size * cores, leg == 0)
        parts = exchange(partial.reshape(back_size, cores, vec_count, tile_width), leg + 1)
        return jnp.sum(parts, axis=0, dtype=jnp.float32)

    def operate(make_blocks, operand):
        mine = lax.cond(
            core == 0,
            functools.partial(chain, 0, make_blocks),
            functools.partial(chain, 2, make_blocks),
            operand,
        )
        return both_cores(mine).reshape(2, cores, vec_count, tile_width)

    def start_blocks(array):
        return array[:, :vec_count]

    def next_blocks(parts):
        return factor * (parts[0] + parts[1])

    parts = operate(start_blocks, packed)
    parts = operate(next_blocks, parts)
    mine = lax.dynamic_index_in_dim(parts, core, 1, keepdims=False)
    return 2.0 * factor * (mine[0] + mine[1]) - kept


def solution(mesh):
    rows, cols = mesh.devices.shape
    pairs = cols // 2
    split = Mesh(mesh.devices.reshape(rows, pairs, 2), ("row", "pair", "core"))
    columns = ("pair", "core")
    in_specs = (
        P(None, (*columns, "row")),
        P("row", columns, None, None, None),
        P("row", columns, None),
        P("row", columns, None),
        P("row", columns, None),
        P("row", columns),
    )
    out_specs = P(None, (*columns, "row"))
    step = functools.partial(body, LEADS)
    return jax.shard_map(step, mesh=split, in_specs=in_specs, out_specs=out_specs, check_vma=False)
```
